256 devices in a mesh: row: 8 (over y, core), col: 32 (over x, z).
Axes of the slice: x: 4, y: 4, z: 8, core: 2. Of those that a mesh axis runs over, the one named last changes fastest.
Arguments:
- columns: float32 [2048, 131072], P(None, ('row', 'col')), may hold values from -6000 to 6000
- seating: int32 [32], replicated, may hold values from 0 to 31, each once
Outputs:
- rotated: float32 [2048, 131072], P(None, ('row', 'col'))
The draws below stay inside these ranges and needn't reach their ends.
All inputs are finite; a program needn't handle non-finite values.
Results may differ from the reference program's by a relative error of at most 0.0001.
Values sent between devices are 32-bit elements; how exact they have to be, the bound alone decides.
No kernel may reach another device: no remote copies, remote signals or barrier semaphores. Data moves between devices by JAX's collectives and lax.ppermute only.
A program may use at most 128 MiB of HBM per device.

```python
import jax
import jax.numpy as jnp
from jax import lax

COLS = 2048
BLOCK = 64
NS_STEPS = 5
BLOCKS = 32
ROWS = 131072
N_COL = 32


def draw_columns(key, part):
    subkeys = jax.random.split(jax.random.fold_in(key, 11), 5)
    noise = jnp.clip(jax.random.normal(subkeys[0], (COLS, ROWS), jnp.float32), -6.0, 6.0)
    ceiling = 10.0
    mixing_scale = 0.5
    col_scale = jnp.exp(jax.random.uniform(subkeys[1], (COLS, 1), jnp.float32, 0.0, 1.0) * jnp.log(ceiling))
    row_scale = jnp.exp(jax.random.uniform(subkeys[2], (1, ROWS), jnp.float32, 0.0, 1.0) * jnp.log(10.0))
    common = jnp.clip(jax.random.normal(subkeys[3], (2, ROWS), jnp.float32), -4.0, 4.0)
    mixing = jnp.clip(jax.random.normal(subkeys[4], (COLS, 2), jnp.float32), -4.0, 4.0) * mixing_scale
    shared = mixing[:, 0:1] * common[0:1, :] + mixing[:, 1:2] * common[1:2, :]
    return col_scale * row_scale * (noise + shared)


def setup_inputs(seed: int = 0) -> dict:
    seeds = jax.random.split(jax.random.key(seed), 3)
    return {
        "columns": draw_columns(jax.random.fold_in(seeds[2], 71), 0),
        "seating": jax.random.permutation(seeds[1], BLOCKS).astype(jnp.int32),
    }


highest = lax.Precision.HIGHEST

def rotation(pair_gram, total_rows):
    pair_width = pair_gram.shape[-1]
    frobenius = jnp.sqrt(lax.optimization_barrier(jnp.sum(pair_gram * pair_gram, axis=(-2, -1), keepdims=True)))
    current = pair_gram / frobenius
    identity = jnp.eye(pair_width, dtype=jnp.float32)
    inverse_root = jnp.broadcast_to(identity, pair_gram.shape)
    for newton_turn in range(NS_STEPS):
        factor = 1.5 * identity - 0.5 * jnp.matmul(inverse_root, current, precision=highest)
        current = jnp.matmul(current, factor, precision=highest)
        inverse_root = jnp.matmul(factor, inverse_root, precision=highest)
    return inverse_root * jnp.sqrt(total_rows / frobenius)

def pair_up(blocks, stride):
    count = blocks.shape[0]
    shaped = blocks.reshape(count // (2 * stride), 2, stride, blocks.shape[1], blocks.shape[2])
    return jnp.concatenate([shaped[:, 0], shaped[:, 1]], axis=2)

def split_pairs(rotated_pairs, stride):
    groups = rotated_pairs.shape[0]
    half_width = rotated_pairs.shape[2] // 2
    shaped = rotated_pairs.reshape(groups, stride, 2, half_width, rotated_pairs.shape[3])
    return jnp.transpose(shaped, (0, 2, 1, 3, 4)).reshape(groups * 2 * stride, half_width, rotated_pairs.shape[3])

def reference(columns, seating):
    block_count = COLS // BLOCK
    current = columns.reshape(block_count, BLOCK, ROWS)[seating]
    for stride in (block_count // N_COL, block_count // 2):
        paired = pair_up(current, stride)
        pair_gram = jnp.einsum('gsam,gsbm->gsab', paired, paired, precision=highest)
        rotate = rotation(pair_gram, float(ROWS))
        moved = jnp.einsum('gsab,gsam->gsbm', rotate, paired, precision=highest)
        current = split_pairs(moved, stride)
    restored = jnp.zeros_like(current).at[seating].set(current)
    return restored.reshape(COLS, ROWS)
```

```python
import jax
import jax.numpy as jnp
from jax import lax
from jax.experimental import pallas as pl
from jax.experimental.pallas import tpu as pltpu
from jax.sharding import PartitionSpec as P

BLOCK = 64
NS_STEPS = 5
NY, NC, NX, NZ = 4, 2, 4, 8
AXES = ("row", "col")
GROUPS = 8
CHUNK = 264
HI = lax.Precision.HIGHEST


def device_permutation(move):
    pairs = []
    for y in range(NY):
        for c in range(NC):
            for x in range(NX):
                for z in range(NZ):
                    ty, tc, tx, tz = move(y, c, x, z)
                    src = (y * NC + c) * NX * NZ + x * NZ + z
                    dst = ((ty % NY) * NC + tc % NC) * NX * NZ + (tx % NX) * NZ + tz % NZ
                    pairs.append((src, dst))
    return pairs


def send(value, move):
    return lax.ppermute(value, AXES, device_permutation(move))


def swap_core(y, c, x, z):
    return y, 1 - c, x, z


def shift_y(d):
    return lambda y, c, x, z: (y + d, c, x, z)


EXCHANGES = (
    lambda y, c, x, z: (y, c, x ^ 1, z),
    lambda y, c, x, z: (y, c, NX - 1 - x, z),
    lambda y, c, x, z: (y, c, x, z ^ 1),
    lambda y, c, x, z: (y, c, x, z ^ 3),
    lambda y, c, x, z: (y, c, x, NZ - 1 - z),
)


def group_at(slot):
    me = lax.axis_index("row")
    y, c = me // NC, me % NC
    core = c if slot >= NY else 1 - c
    return lax.rem(y + slot % NY, NY) * NC + core


def seats_of(group):
    return (2 * group, 2 * group + 1, 2 * group + 16, 2 * group + 17)


def indices(shape):
    return (
        lax.broadcasted_iota(jnp.int32, shape, 0),
        lax.broadcasted_iota(jnp.int32, shape, 1),
    )


def fold(upper, lower):
    i, j = indices(upper.shape)
    diagonal = jnp.sum(jnp.where(i == j, lower, 0.0), axis=0, keepdims=True)
    return jnp.where(i <= j, upper, lower), diagonal


def unfold(folded, diagonal):
    i, j = indices(folded.shape)
    flipped = folded.T
    first = jnp.where(i <= j, folded, flipped)
    second = jnp.where(i > j, folded, jnp.where(i == j, diagonal, flipped))
    return first, second


def split2(value):
    high = value.astype(jnp.bfloat16)
    low = (value - high.astype(jnp.float32)).astype(jnp.bfloat16)
    return high, low


def dot_t(a, b):
    return lax.dot_general(a, b, (((1,), (1,)), ((), ())), preferred_element_type=jnp.float32)


def gram_kernel(seating, columns, away, home, panel, sems):
    def copies(slot):
        group = group_at(slot)
        return [
            pltpu.make_async_copy(
                columns.at[pl.ds(pl.multiple_of(seating[seat] * BLOCK, BLOCK), BLOCK), :],
                panel.at[slot, pl.ds(k * BLOCK, BLOCK), :],
                sems.at[slot, k],
            )
            for k, seat in enumerate(seats_of(group))
        ]

    started = [copies(slot) for slot in range(GROUPS)]
    for slot in range(GROUPS):
        for copy in started[slot]:
            copy.start()
    for slot in range(GROUPS):
        for copy in started[slot]:
            copy.wait()
        high, low = split2(panel[slot])
        cross = dot_t(high, low)
        gram = dot_t(high, high) + cross + dot_t(low, high)
        folded, diagonal = fold(gram[:128, :128], gram[128:, 128:])
        out = away if slot < NY else home
        out[slot % NY, 0:128, :] = gram[:128, 128:]
        out[slot % NY, 128:256, :] = folded
        out[slot % NY, 256:264, :] = jnp.broadcast_to(diagonal, (8, 128))


def mm(a, b):
    return jnp.dot(a, b, precision=HI, preferred_element_type=jnp.float32)


def rotations(grams, total_rows):
    i, j = indices((128, 128))
    identity = jnp.where(i == j, 1.0, 0.0).astype(jnp.float32)
    norms = [jnp.sqrt(jnp.sum(g * g)) for g in grams]
    currents = [g / n for g, n in zip(grams, norms)]
    factors = [1.5 * identity - 0.5 * y for y in currents]
    currents = [mm(y, f) for y, f in zip(currents, factors)]
    roots = factors
    for turn in range(1, NS_STEPS):
        products = [mm(r, y) for r, y in zip(roots, currents)]
        factors = [1.5 * identity - 0.5 * p for p in products]
        if turn + 1 < NS_STEPS:
            currents = [mm(y, f) for y, f in zip(currents, factors)]
        roots = [mm(f, r) for f, r in zip(factors, roots)]
    return [r * jnp.sqrt(total_rows / n) for r, n in zip(roots, norms)]


def stack_rows(va, vb, half):
    zero = jnp.zeros((BLOCK, 128), jnp.float32)
    rows = slice(half * BLOCK, half * BLOCK + BLOCK)
    return jnp.concatenate(
        [
            jnp.concatenate([va[rows], zero], axis=1),
            jnp.concatenate([zero, vb[rows]], axis=1),
        ],
        axis=0,
    )


def rotation_kernel(total_rows, mine, theirs, out):
    whole = mine[...] + theirs[...]
    cross = whole[0:128]
    first, second = unfold(whole[128:256], whole[256:257])
    gram = jnp.concatenate(
        [
            jnp.concatenate([first, cross], axis=1),
            jnp.concatenate([cross.T, second], axis=1),
        ],
        axis=0,
    )
    va, vb = rotations([first, second], total_rows)
    lower = stack_rows(va, vb, 0)
    upper = stack_rows(va, vb, 1)

    def turned(q):
        return lax.dot_general(
            mm(q, gram), q, (((1,), (1,)), ((), ())), precision=HI, preferred_element_type=jnp.float32
        )

    vc, vd = rotations([turned(lower), turned(upper)], total_rows)
    ab, b_diagonal = fold(va, vb)
    cd, d_diagonal = fold(vc, vd)
    out[0:128] = ab
    out[128:256] = cd
    i, _ = indices((8, 128))
    out[256:264] = jnp.where(i == 0, b_diagonal, d_diagonal)


def apply_kernel(seating, columns, *refs):
    turns = refs[:GROUPS]
    out, panel, result, in_sems, out_sems = refs[GROUPS:]

    def copies(slot):
        group = group_at(slot)
        ins, outs = [], []
        for k, seat in enumerate(seats_of(group)):
            rows = pl.ds(pl.multiple_of(seating[seat] * BLOCK, BLOCK), BLOCK)
            ins.append(
                pltpu.make_async_copy(
                    columns.at[rows, :], panel.at[slot, pl.ds(k * BLOCK, BLOCK), :], in_sems.at[slot, k]
                )
            )
        for k, seat in enumerate((2 * group, 2 * group + 16, 2 * group + 1, 2 * group + 17)):
            rows = pl.ds(pl.multiple_of(seating[seat] * BLOCK, BLOCK), BLOCK)
            outs.append(
                pltpu.make_async_copy(
                    result.at[slot, pl.ds(k * BLOCK, BLOCK), :], out.at[rows, :], out_sems.at[slot, k]
                )
            )
        return ins, outs

    order = list(range(NY, GROUPS)) + list(range(NY))
    started = {slot: copies(slot) for slot in order}
    for slot in order:
        for copy in started[slot][0]:
            copy.start()
    for slot in order:
        turn = turns[slot][...]
        va, vb = unfold(turn[0:128], turn[256:257])
        vc, vd = unfold(turn[128:256], turn[257:258])
        rotate = jnp.concatenate([mm(vc, stack_rows(va, vb, 0)), mm(vd, stack_rows(va, vb, 1))], axis=0)
        for copy in started[slot][0]:
            copy.wait()
        result[slot] = mm(rotate, panel[slot])
        for copy in started[slot][1]:
            copy.start()
    for slot in order:
        for copy in started[slot][1]:
            copy.wait()


def body(columns, seating):
    rows_here = columns.shape[1]
    total_rows = float(rows_here * lax.axis_size(AXES))
    smem = pl.BlockSpec(memory_space=pltpu.SMEM)
    hbm = pl.BlockSpec(memory_space=pl.ANY)
    vmem = pl.BlockSpec(memory_space=pltpu.VMEM)
    chunk = jax.ShapeDtypeStruct((CHUNK, 128), jnp.float32)
    quarter = jax.ShapeDtypeStruct((NY, CHUNK, 128), jnp.float32)

    away, home = pl.pallas_call(
        gram_kernel,
        out_shape=(quarter, quarter),
        in_specs=[smem, hbm],
        out_specs=(vmem, vmem),
        scratch_shapes=[
            pltpu.VMEM((GROUPS, 256, rows_here), jnp.float32),
            pltpu.SemaphoreType.DMA((GROUPS, 4)),
        ],
        name="gram",
    )(seating, columns)

    here = home + send(away, swap_core)
    arrived = [send(here[d], shift_y(d)) for d in range(1, NY)]
    total = here[0] + arrived[0] + arrived[1] + arrived[2]
    for exchange in EXCHANGES[:-1]:
        total = total + send(total, exchange)
    other = send(total, EXCHANGES[-1])

    turn = pl.pallas_call(
        lambda *refs: rotation_kernel(total_rows, *refs),
        out_shape=chunk,
        in_specs=[vmem, vmem],
        out_specs=vmem,
        name="rotation",
    )(total, other)

    near = [turn] + [send(turn, shift_y(-d)) for d in range(1, NY)]
    far = [send(t, swap_core) for t in near]

    return pl.pallas_call(
        apply_kernel,
        out_shape=jax.ShapeDtypeStruct(columns.shape, columns.dtype),
        in_specs=[smem, hbm] + [vmem] * GROUPS,
        out_specs=hbm,
        scratch_shapes=[
            pltpu.VMEM((GROUPS, 256, rows_here), jnp.float32),
            pltpu.VMEM((GROUPS, 256, rows_here), jnp.float32),
            pltpu.SemaphoreType.DMA((GROUPS, 4)),
            pltpu.SemaphoreType.DMA((GROUPS, 4)),
        ],
        name="apply",
    )(seating, columns, *far, *near)


def solution(mesh):
    in_specs = (P(None, AXES), P())
    out_specs = P(None, AXES)
    return jax.shard_map(body, mesh=mesh, in_specs=in_specs, out_specs=out_specs, check_vma=False)
```

```python
import functools

import jax
import jax.numpy as jnp
from jax import lax
from jax.experimental import pallas as pl
from jax.experimental.pallas import tpu as pltpu
from jax.sharding import PartitionSpec as P


BLOCK = 64
NS_STEPS = 5
NY, NC, NX, NZ = 4, 2, 4, 8
AXES = ("row", "col")
SPREAD = 4
CHUNK = 264
CUT = 136
MIB = 1 << 20
GRAM_MIB = 8
SPLIT_MIB = 8


def device_permutation(move):
    pairs = []
    for y in range(NY):
        for c in range(NC):
            for x in range(NX):
                for z in range(NZ):
                    ty, tc, tx, tz = move(y, c, x, z)
                    src = (y * NC + c) * NX * NZ + x * NZ + z
                    dst = ((ty % NY) * NC + tc % NC) * NX * NZ + (tx % NX) * NZ + tz % NZ
                    pairs.append((src, dst))
    return pairs


def send(value, move):
    return lax.ppermute(value, AXES, device_permutation(move))


def swap_core(y, c, x, z):
    return y, 1 - c, x, z


def shift(d):
    return lambda y, c, x, z: (y + d, c, x, z) if c == 0 else (y, c, x + d, z)


def pairings(axis):
    return {
        "x": (lambda y, c, x, z: (y, c, x ^ 1, z), lambda y, c, x, z: (y, c, NX - 1 - x, z)),
        "y": (lambda y, c, x, z: (y ^ 1, c, x, z), lambda y, c, x, z: (NY - 1 - y, c, x, z)),
        "z": (
            lambda y, c, x, z: (y, c, x, z ^ 1),
            lambda y, c, x, z: (y, c, x, z ^ 3),
            lambda y, c, x, z: (y, c, x, NZ - 1 - z),
        ),
    }[axis]


def by_core(first, second):
    return lambda y, c, x, z: first(y, c, x, z) if c == 0 else second(y, c, x, z)


EXCHANGES = tuple(
    by_core(first, second)
    for first, second in (
        *zip(pairings("x") + pairings("z"), pairings("z") + pairings("y")),
        *zip(pairings("z") + pairings("x"), pairings("y") + pairings("z")),
    )
)


def group_at(slot):
    row = lax.axis_index("row")
    y, c = row // NC, row % NC
    x = lax.axis_index("col") // NZ
    mine = slot >= SPREAD
    place = y * (1 - c) + x * c if mine else x * (1 - c) + y * c
    return lax.rem(place + slot % SPREAD, SPREAD) * NC + (c if mine else 1 - c)


def seat_rows(seating, seat):
    return pl.ds(pl.multiple_of(seating[seat] * BLOCK, BLOCK), BLOCK)


def blocks_of(slot):
    group = group_at(slot)
    return 2 * group, 2 * group + 1, 2 * group + 16, 2 * group + 17


def indices(shape):
    return (
        lax.broadcasted_iota(jnp.int32, shape, 0),
        lax.broadcasted_iota(jnp.int32, shape, 1),
    )


def fold(upper, lower):
    i, j = indices(upper.shape)
    diagonal = jnp.sum(jnp.where(i == j, lower, 0.0), axis=0, keepdims=True)
    return jnp.where(i <= j, upper, lower), diagonal


def unfold(folded, diagonal):
    i, j = indices(folded.shape)
    flipped = folded.T
    first = jnp.where(i <= j, folded, flipped)
    second = jnp.where(i > j, folded, jnp.where(i == j, diagonal, flipped))
    return first, second


def pieces(value):
    high = value.astype(jnp.bfloat16)
    rest = value - high.astype(jnp.float32)
    middle = rest.astype(jnp.bfloat16)
    low = (rest - middle.astype(jnp.float32)).astype(jnp.bfloat16)
    return high, middle, low


def wide(parts, axis):
    high, middle, low = parts
    if axis == 1:
        return jnp.concatenate([high, high, middle, middle, high, low], axis=1)
    return jnp.concatenate([high, middle, high, middle, low, high], axis=0)


def mm(a, b):
    return jnp.dot(wide(a, 1), wide(b, 0), preferred_element_type=jnp.float32)


def dot_t(a, b):
    return lax.dot_general(a, b, (((1,), (1,)), ((), ())), preferred_element_type=jnp.float32)


def mm_t(a, b):
    left = wide(a, 1)
    high, middle, low = b
    return dot_t(left, jnp.concatenate([high, middle, high, middle, low, high], axis=1))


def gram_kernel(first_slot, whole, seating, columns, *outs):
    for k in range(SPREAD):
        seats = blocks_of(first_slot + k)
        value = jnp.concatenate([columns[seat_rows(seating, seat), :] for seat in seats], axis=0)
        high = value.astype(jnp.bfloat16)
        low = (value - high.astype(jnp.float32)).astype(jnp.bfloat16)
        both = dot_t(jnp.concatenate([high, low], axis=0), high)
        even, odd = both[:256], both[256:]
        upper = even[:128, :128] + odd[:128, :128] + odd[:128, :128].T
        cross = even[:128, 128:] + odd[:128, 128:] + odd[128:, :128].T
        lower = even[128:, 128:] + odd[128:, 128:] + odd[128:, 128:].T
        folded, diagonal = fold(upper, lower)
        out = outs[0].at[k] if whole else outs[k]
        out[0:128, :] = folded
        out[128:136, :] = jnp.broadcast_to(diagonal, (8, 128))
        out[136:264, :] = cross


def rotations(grams, total_rows):
    i, j = indices((128, 128))
    identity = jnp.where(i == j, 1.0, 0.0).astype(jnp.float32)
    squares = [jnp.sum(jnp.sum(g * g, axis=0, keepdims=True), axis=1, keepdims=True) for g in grams]
    inverses = [1.0 / jnp.sqrt(s) for s in squares]
    currents = [g * v for g, v in zip(grams, inverses)]
    factors = [1.5 * identity - 0.5 * y for y in currents]
    factors = [pieces(f) for f in factors]
    currents = [mm(pieces(y), f) for y, f in zip(currents, factors)]
    root_pieces = factors
    for turn in range(1, NS_STEPS):
        current_pieces = [pieces(y) for y in currents]
        products = [mm(r, y) for r, y in zip(root_pieces, current_pieces)]
        factors = [pieces(1.5 * identity - 0.5 * p) for p in products]
        if turn + 1 < NS_STEPS:
            joint = [
                mm(f, tuple(jnp.concatenate([p, q], axis=1) for p, q in zip(y, r)))
                for f, y, r in zip(factors, current_pieces, root_pieces)
            ]
            currents = [j[:, :128] for j in joint]
            root_pieces = [pieces(j[:, 128:]) for j in joint]
        else:
            roots = [mm(f, r) for f, r in zip(factors, root_pieces)]
    return [r * jnp.sqrt(total_rows * v) for r, v in zip(roots, inverses)]


def stack_rows(va, vb, half):
    zero = jnp.zeros((BLOCK, 128), va.dtype)
    rows = slice(half * BLOCK, half * BLOCK + BLOCK)
    return jnp.concatenate(
        [
            jnp.concatenate([va[rows], zero], axis=1),
            jnp.concatenate([zero, vb[rows]], axis=1),
        ],
        axis=0,
    )


def rotation_kernel(total_rows, straight, crossed, out):
    first, second = unfold(straight[0:128], straight[128:129])
    cross = crossed[...]
    va, vb = rotations([first, second], total_rows)
    pa, pb = pieces(va), pieces(vb)
    top = mm(pa, pieces(jnp.concatenate([first, cross], axis=1)))
    bottom = mm(pb, pieces(jnp.concatenate([cross.T, second], axis=1)))
    grams = []
    for half in range(2):
        rows = slice(half * BLOCK, half * BLOCK + BLOCK)
        left = pieces(jnp.concatenate([top[rows], bottom[rows]], axis=0))
        right = tuple(stack_rows(p, q, half) for p, q in zip(pa, pb))
        grams.append(mm_t(left, right))
    vc, vd = rotations(grams, total_rows)
    ab, b_diagonal = fold(va, vb)
    cd, d_diagonal = fold(vc, vd)
    out[0:128] = ab
    out[128:256] = cd
    i, _ = indices((8, 128))
    out[256:264] = jnp.where(i == 0, b_diagonal, d_diagonal)


def split_kernel(seating, columns, *outs):
    for slot in range(2 * SPREAD):
        for n, seat in enumerate(blocks_of(slot)):
            for part, value in enumerate(pieces(columns[seat_rows(seating, seat), :])):
                outs[slot][pl.ds(part * 256 + n * BLOCK, BLOCK), :] = value


def turned(turn, panel):
    va, vb = unfold(turn[0:128], turn[256:257])
    vc, vd = unfold(turn[128:256], turn[257:258])
    pa, pb = pieces(va), pieces(vb)
    rotate = jnp.concatenate(
        [
            mm(pieces(v), tuple(stack_rows(p, q, half) for p, q in zip(pa, pb)))
            for half, v in enumerate((vc, vd))
        ],
        axis=0,
    )
    return mm(pieces(rotate), (panel[0:256], panel[256:512], panel[512:768]))


def near_kernel(*refs):
    count = len(refs) // 3
    turns, panels, outs = refs[:count], refs[count : 2 * count], refs[2 * count :]
    for turn, panel, out in zip(turns, panels, outs):
        out[...] = turned(turn[...], panel[...])


def far_kernel(seating, *refs):
    turns, panels, done = refs[:SPREAD], refs[SPREAD : 2 * SPREAD], refs[2 * SPREAD : 3 * SPREAD]
    out, result, sems = refs[3 * SPREAD :]

    def stores(slot, value):
        group = group_at(slot)
        return [
            pltpu.make_async_copy(
                value.at[pl.ds(n * BLOCK, BLOCK), :], out.at[seat_rows(seating, seat), :], sems.at[slot, n]
            )
            for n, seat in enumerate((2 * group, 2 * group + 16, 2 * group + 1, 2 * group + 17))
        ]

    copies = []
    for k in range(SPREAD):
        copies += stores(SPREAD + k, done[k])
    for copy in copies:
        copy.start()
    for k in range(SPREAD):
        result[k] = turned(turns[k][...], panels[k][...])
        for copy in stores(k, result.at[k]):
            copy.start()
            copies.append(copy)
    for copy in copies:
        copy.wait()


def exchange(value, order):
    for axis in order:
        value = value + send(value, EXCHANGES[axis])
    return value


def steps(columns, seating):
    rows_here = columns.shape[1]
    total_rows = float(rows_here * lax.axis_size(AXES))
    smem = pl.BlockSpec(memory_space=pltpu.SMEM)
    hbm = pl.BlockSpec(memory_space=pltpu.MemorySpace.HBM)
    vmem = pl.BlockSpec(memory_space=pltpu.VMEM)
    chunk = jax.ShapeDtypeStruct((CHUNK, 128), jnp.float32)
    quarter = jax.ShapeDtypeStruct((SPREAD, CHUNK, 128), jnp.float32)
    panel_flops = 2 * 256 * 256 * rows_here

    def params(mib):
        return pltpu.CompilerParams(vmem_limit_bytes=mib * MIB)

    def cost(flops, moved):
        return pl.CostEstimate(flops=flops, bytes_accessed=moved, transcendentals=0)

    def gram(first_slot, whole):
        return pl.pallas_call(
            functools.partial(gram_kernel, first_slot, whole),
            out_shape=quarter if whole else (chunk,) * SPREAD,
            in_specs=[smem, vmem],
            out_specs=vmem if whole else (vmem,) * SPREAD,
            compiler_params=params(GRAM_MIB),
            cost_estimate=cost(2 * SPREAD * panel_flops, 2 * MIB),
            name="gram_away" if whole else "gram_home",
        )(seating, columns)

    away = gram(0, True)
    passed = send(away, swap_core)
    home = gram(SPREAD, False)
    here = [home[d] + passed[d] for d in range(SPREAD)]

    later, here = lax.optimization_barrier((seating, here))
    panels = pl.pallas_call(
        split_kernel,
        out_shape=(jax.ShapeDtypeStruct((768, rows_here), jnp.bfloat16),) * (2 * SPREAD),
        in_specs=[smem, vmem],
        out_specs=(vmem,) * (2 * SPREAD),
        compiler_params=params(SPLIT_MIB),
        cost_estimate=cost(0, 10 * MIB),
        name="split",
    )(later, columns)
    arrived = []
    for d in range(1, SPREAD):
        arrived.append(send(here[d], shift(d)))
    total = here[0] + arrived[0] + arrived[1] + arrived[2]
    total, panels = lax.optimization_barrier((total, panels))

    halves = [exchange(total[:CUT], (0, 1, 2, 3, 4)), exchange(total[CUT:], (5, 6, 7, 8, 9))]
    turn = pl.pallas_call(
        functools.partial(rotation_kernel, total_rows),
        out_shape=chunk,
        in_specs=[vmem, vmem],
        out_specs=vmem,
        compiler_params=params(8),
        name="rotation",
    )(*halves)

    def apply(slots, turns):
        count = len(slots)
        return pl.pallas_call(
            near_kernel,
            out_shape=(jax.ShapeDtypeStruct((256, rows_here), jnp.float32),) * count,
            in_specs=[vmem] * (2 * count),
            out_specs=(vmem,) * count,
            compiler_params=params(8),
            cost_estimate=cost(6 * count * panel_flops, count * MIB),
            name="apply_near",
        )(*turns, *[panels[slot] for slot in slots])

    near = [turn]
    for d in range(1, SPREAD):
        near.append(send(turn, shift(-d)))
    far = []
    for d in range(SPREAD):
        far.append(send(near[d], swap_core))
    done = apply((4,), near[:1])
    done += apply((5,), near[1:2])
    done += apply((6, 7), near[2:])
    return pl.pallas_call(
        far_kernel,
        out_shape=jax.ShapeDtypeStruct(columns.shape, columns.dtype),
        in_specs=[smem] + [vmem] * (3 * SPREAD),
        out_specs=hbm,
        scratch_shapes=[
            pltpu.VMEM((SPREAD, 256, rows_here), jnp.float32),
            pltpu.SemaphoreType.DMA((2 * SPREAD, 4)),
        ],
        compiler_params=params(10),
        name="apply_far",
    )(seating, *far, *[panels[slot] for slot in range(SPREAD)], *done)


def solution(mesh):
    in_specs = (P(None, AXES), P())
    out_specs = P(None, AXES)
    return jax.shard_map(steps, mesh=mesh, in_specs=in_specs, out_specs=out_specs, check_vma=False)
```

```python
import functools

import jax
import jax.numpy as jnp
from jax import lax
from jax.experimental import pallas as pl
from jax.experimental.pallas import tpu as pltpu
from jax.sharding import PartitionSpec as P


BLOCK = 64
NS_STEPS = 5
NY, NC, NX, NZ = 4, 2, 4, 8
AXES = ("row", "col")
SPREAD = 4
CHUNK = 264
CUT = 136
FAR_FIRST = (2, 1, 3, 0)
MIB = 1 << 20


def device_permutation(move):
    pairs = []
    for y in range(NY):
        for c in range(NC):
            for x in range(NX):
                for z in range(NZ):
                    ty, tc, tx, tz = move(y, c, x, z)
                    src = (y * NC + c) * NX * NZ + x * NZ + z
                    dst = ((ty % NY) * NC + tc % NC) * NX * NZ + (tx % NX) * NZ + tz % NZ
                    pairs.append((src, dst))
    return pairs


def send(value, move):
    return lax.ppermute(value, AXES, device_permutation(move))


def swap_core(y, c, x, z):
    return y, 1 - c, x, z


def shift(d):
    return lambda y, c, x, z: (y + d, c, x, z) if c == 0 else (y, c, x + d, z)


def pairings(axis):
    return {
        "x": (lambda y, c, x, z: (y, c, x ^ 1, z), lambda y, c, x, z: (y, c, NX - 1 - x, z)),
        "y": (lambda y, c, x, z: (y ^ 1, c, x, z), lambda y, c, x, z: (NY - 1 - y, c, x, z)),
        "z": (
            lambda y, c, x, z: (y, c, x, z ^ 1),
            lambda y, c, x, z: (y, c, x, z ^ 3),
            lambda y, c, x, z: (y, c, x, NZ - 1 - z),
        ),
    }[axis]


def by_core(first, second):
    return lambda y, c, x, z: first(y, c, x, z) if c == 0 else second(y, c, x, z)


EXCHANGES = tuple(by_core(first, second) for first, second in zip(pairings("z") + pairings("x"), pairings("z") + pairings("y")))
EVEN_ORDER = (0, 1, 2, 3, 4)
ODD_ORDER = (3, 4, 0, 1, 2)


def group_at(slot):
    row = lax.axis_index("row")
    y, c = row // NC, row % NC
    x = lax.axis_index("col") // NZ
    mine = slot >= SPREAD
    place = y * (1 - c) + x * c if mine else x * (1 - c) + y * c
    return lax.rem(place + slot % SPREAD, SPREAD) * NC + (c if mine else 1 - c)


def seat_rows(seating, seat):
    return pl.ds(pl.multiple_of(seating[seat] * BLOCK, BLOCK), BLOCK)


def blocks_of(slot):
    group = group_at(slot)
    return 2 * group, 2 * group + 1, 2 * group + 16, 2 * group + 17


def indices(shape):
    return (
        lax.broadcasted_iota(jnp.int32, shape, 0),
        lax.broadcasted_iota(jnp.int32, shape, 1),
    )


def fold(upper, lower):
    i, j = indices(upper.shape)
    diagonal = jnp.sum(jnp.where(i == j, lower, 0.0), axis=0, keepdims=True)
    return jnp.where(i <= j, upper, lower), diagonal


def unfold(folded, diagonal):
    i, j = indices(folded.shape)
    flipped = folded.T
    first = jnp.where(i <= j, folded, flipped)
    second = jnp.where(i > j, folded, jnp.where(i == j, diagonal, flipped))
    return first, second


def pieces(value):
    high = value.astype(jnp.bfloat16)
    rest = value - high.astype(jnp.float32)
    middle = rest.astype(jnp.bfloat16)
    low = (rest - middle.astype(jnp.float32)).astype(jnp.bfloat16)
    return high, middle, low


def wide(parts, axis):
    high, middle, low = parts
    if axis == 1:
        return jnp.concatenate([high, high, middle, middle, high, low], axis=1)
    return jnp.concatenate([high, middle, high, middle, low, high], axis=0)


def mm(a, b):
    return jnp.dot(wide(a, 1), wide(b, 0), preferred_element_type=jnp.float32)


def dot_t(a, b):
    return lax.dot_general(a, b, (((1,), (1,)), ((), ())), preferred_element_type=jnp.float32)


def mm_t(a, b):
    left = wide(a, 1)
    high, middle, low = b
    return dot_t(left, jnp.concatenate([high, middle, high, middle, low, high], axis=1))


def away_kernel(seating, columns, *refs):
    outs, (panel, sems) = refs[:-2], refs[-2:]
    copies = [
        [
            pltpu.make_async_copy(
                columns.at[seat_rows(seating, seat), :], panel.at[slot, pl.ds(n * BLOCK, BLOCK), :], sems.at[slot, n]
            )
            for n, seat in enumerate(blocks_of(slot))
        ]
        for slot in range(2 * SPREAD)
    ]
    for group in copies:
        for copy in group:
            copy.start()
    for group in copies[:SPREAD]:
        for copy in group:
            copy.wait()
    for k, out in enumerate(outs):
        folded_gram(panel[k], out)
    for group in copies[SPREAD:]:
        for copy in group:
            copy.wait()


def home_kernel(panel, *outs):
    for k, out in enumerate(outs):
        folded_gram(panel[SPREAD + k], out)


def folded_gram(value, out):
    high = value.astype(jnp.bfloat16)
    low = (value - high.astype(jnp.float32)).astype(jnp.bfloat16)
    both = dot_t(jnp.concatenate([high, low], axis=0), high)
    even, odd = both[:256], both[256:]
    upper = even[:128, :128] + odd[:128, :128] + odd[:128, :128].T
    cross = even[:128, 128:] + odd[:128, 128:] + odd[128:, :128].T
    lower = even[128:, 128:] + odd[128:, 128:] + odd[128:, 128:].T
    folded, diagonal = fold(upper, lower)
    out[0:128, :] = folded
    out[128:136, :] = jnp.broadcast_to(diagonal, (8, 128))
    out[136:264, :] = cross


def rotations(grams, total_rows):
    i, j = indices((128, 128))
    identity = jnp.where(i == j, 1.0, 0.0).astype(jnp.float32)
    squares = [jnp.sum(jnp.sum(g * g, axis=0, keepdims=True), axis=1, keepdims=True) for g in grams]
    inverses = [1.0 / jnp.sqrt(s) for s in squares]
    currents = [g * v for g, v in zip(grams, inverses)]
    factors = [1.5 * identity - 0.5 * y for y in currents]
    factors = [pieces(f) for f in factors]
    currents = [mm(pieces(y), f) for y, f in zip(currents, factors)]
    root_pieces = factors
    for turn in range(1, NS_STEPS):
        current_pieces = [pieces(y) for y in currents]
        products = [mm(r, y) for r, y in zip(root_pieces, current_pieces)]
        factors = [pieces(1.5 * identity - 0.5 * p) for p in products]
        if turn + 1 < NS_STEPS:
            joint = [
                mm(f, tuple(jnp.concatenate([p, q], axis=1) for p, q in zip(y, r)))
                for f, y, r in zip(factors, current_pieces, root_pieces)
            ]
            currents = [j[:, :128] for j in joint]
            root_pieces = [pieces(j[:, 128:]) for j in joint]
        else:
            roots = [mm(f, r) for f, r in zip(factors, root_pieces)]
    return [r * jnp.sqrt(total_rows * v) for r, v in zip(roots, inverses)]


def stack_rows(va, vb, half):
    zero = jnp.zeros((BLOCK, 128), va.dtype)
    rows = slice(half * BLOCK, half * BLOCK + BLOCK)
    return jnp.concatenate(
        [
            jnp.concatenate([va[rows], zero], axis=1),
            jnp.concatenate([zero, vb[rows]], axis=1),
        ],
        axis=0,
    )


def even_kernel(total_rows, straight, out):
    first, second = unfold(straight[0:128], straight[128:129])
    va, vb = rotations([first, second], total_rows)
    out[0:128], diagonal = fold(va, vb)
    out[128:136] = jnp.broadcast_to(diagonal, (8, 128))


def odd_kernel(total_rows, straight, turned_even, crossed, out):
    first, second = unfold(straight[0:128], straight[128:129])
    va, vb = unfold(turned_even[0:128], turned_even[128:129])
    cross = crossed[...]
    pa, pb = pieces(va), pieces(vb)
    top = mm(pa, pieces(jnp.concatenate([first, cross], axis=1)))
    bottom = mm(pb, pieces(jnp.concatenate([cross.T, second], axis=1)))
    grams = []
    for half in range(2):
        rows = slice(half * BLOCK, half * BLOCK + BLOCK)
        left = pieces(jnp.concatenate([top[rows], bottom[rows]], axis=0))
        right = tuple(stack_rows(p, q, half) for p, q in zip(pa, pb))
        grams.append(mm_t(left, right))
    vc, vd = rotations(grams, total_rows)
    out[0:128] = turned_even[0:128]
    out[128:256], d_diagonal = fold(vc, vd)
    i, _ = indices((8, 128))
    out[256:264] = jnp.where(i == 0, turned_even[128:136], d_diagonal)


def split_kernel(panel, *outs):
    for slot in range(2 * SPREAD):
        for part, value in enumerate(pieces(panel[slot])):
            outs[slot][pl.ds(part * 256, 256), :] = value


def turned(turn, panel):
    va, vb = unfold(turn[0:128], turn[256:257])
    vc, vd = unfold(turn[128:256], turn[257:258])
    pa, pb = pieces(va), pieces(vb)
    rotate = jnp.concatenate(
        [
            mm(pieces(v), tuple(stack_rows(p, q, half) for p, q in zip(pa, pb)))
            for half, v in enumerate((vc, vd))
        ],
        axis=0,
    )
    return mm(pieces(rotate), (panel[0:256], panel[256:512], panel[512:768]))


def near_kernel(*refs):
    count = len(refs) // 3
    turns, panels, outs = refs[:count], refs[count : 2 * count], refs[2 * count :]
    for turn, panel, out in zip(turns, panels, outs):
        out[...] = turned(turn[...], panel[...])


def far_kernel(last, early, seating, *refs):
    count = len(last)
    turns, panels, done = refs[:count], refs[count : 2 * count], refs[2 * count : -5]
    out, result, order, sems, order_sem = refs[-5:]
    fetch = pltpu.make_async_copy(seating, order, order_sem)
    fetch.start()

    def stores(slot, value):
        group = group_at(slot)
        return [
            pltpu.make_async_copy(
                value.at[pl.ds(n * BLOCK, BLOCK), :], out.at[seat_rows(order, seat), :], sems.at[slot, n]
            )
            for n, seat in enumerate((2 * group, 2 * group + 16, 2 * group + 1, 2 * group + 17))
        ]

    copies = []
    for k, slot in enumerate(last):
        result[k] = turned(turns[k][...], panels[k][...])
        if k == 0:
            fetch.wait()
            for waiting, value in zip(early, done):
                copies += stores(waiting, value)
            for copy in copies:
                copy.start()
        for copy in stores(slot, result.at[k]):
            copy.start()
            copies.append(copy)
    for copy in copies:
        copy.wait()


def exchange(value, order):
    for axis in order:
        value = value + send(value, EXCHANGES[axis])
    return value


def steps(columns, seating):
    columns = pltpu.with_memory_space_constraint(columns, pltpu.MemorySpace.HBM)
    seating = pltpu.with_memory_space_constraint(seating, pltpu.MemorySpace.HBM)
    rows_here = columns.shape[1]
    total_rows = float(rows_here * lax.axis_size(AXES))
    smem = pl.BlockSpec(memory_space=pltpu.SMEM)
    hbm = pl.BlockSpec(memory_space=pltpu.MemorySpace.HBM)
    vmem = pl.BlockSpec(memory_space=pltpu.VMEM)
    chunk = jax.ShapeDtypeStruct((CHUNK, 128), jnp.float32)
    panel_flops = 2 * 256 * 256 * rows_here

    def params(mib):
        return pltpu.CompilerParams(vmem_limit_bytes=mib * MIB)

    def cost(flops, moved):
        return pl.CostEstimate(flops=flops, bytes_accessed=moved, transcendentals=0)

    *away, panel = pl.pallas_call(
        away_kernel,
        out_shape=(*(chunk,) * SPREAD, jax.ShapeDtypeStruct((2 * SPREAD, 256, rows_here), jnp.float32)),
        in_specs=[smem, hbm],
        out_specs=(vmem,) * (SPREAD + 1),
        scratch_shapes=[pltpu.SemaphoreType.DMA((2 * SPREAD, 4))],
        compiler_params=params(8),
        name="gram_away",
    )(seating, columns)
    passed = {}
    for d in FAR_FIRST:
        passed[d] = send(away[d], swap_core)
    home = pl.pallas_call(
        home_kernel,
        out_shape=(chunk,) * SPREAD,
        in_specs=[vmem],
        out_specs=(vmem,) * SPREAD,
        compiler_params=params(8),
        cost_estimate=cost(2 * SPREAD * panel_flops, 2 * MIB),
        name="gram_home",
    )(panel)
    here = []
    for d in range(SPREAD):
        here.append(home[d] + passed[d])

    panel, here[2] = lax.optimization_barrier((panel, here[2]))
    panels = pl.pallas_call(
        split_kernel,
        out_shape=(jax.ShapeDtypeStruct((768, rows_here), jnp.bfloat16),) * (2 * SPREAD),
        in_specs=[vmem],
        out_specs=(vmem,) * (2 * SPREAD),
        compiler_params=params(8),
        cost_estimate=cost(0, 10 * MIB),
        name="split",
    )(panel)
    arrived = []
    for d in range(1, SPREAD):
        arrived.append(send(here[d], shift(d)))
    total = here[0] + arrived[0] + arrived[1] + arrived[2]
    total, panels = lax.optimization_barrier((total, panels))

    straight = exchange(total[:CUT], EVEN_ORDER)
    crossed = exchange(total[CUT:], ODD_ORDER)
    even = pl.pallas_call(
        functools.partial(even_kernel, total_rows),
        out_shape=jax.ShapeDtypeStruct((CUT, 128), jnp.float32),
        in_specs=[vmem],
        out_specs=vmem,
        compiler_params=params(8),
        cost_estimate=cost(300 * 128**3, MIB),
        name="rotation_even",
    )(straight)
    turn = pl.pallas_call(
        functools.partial(odd_kernel, total_rows),
        out_shape=chunk,
        in_specs=[vmem] * 3,
        out_specs=vmem,
        compiler_params=params(8),
        name="rotation_odd",
    )(straight, even, crossed)

    def apply(slots, turns):
        count = len(slots)
        return pl.pallas_call(
            near_kernel,
            out_shape=(jax.ShapeDtypeStruct((256, rows_here), jnp.float32),) * count,
            in_specs=[vmem] * (2 * count),
            out_specs=(vmem,) * count,
            compiler_params=params(8),
            cost_estimate=cost(6 * count * panel_flops, count * MIB),
            name="apply_near",
        )(*turns, *[panels[slot] for slot in slots])

    near = [turn]
    for d in range(1, SPREAD):
        near.append(send(turn, shift(-d)))
    far = []
    for d in range(SPREAD):
        far.append(send(near[d], swap_core))
    early = []
    for slots, turns in (
        ((4,), near[:1]), ((0,), far[:1]), ((5,), near[1:2]), ((7, 6), [near[3], near[2]])
    ):
        early += [(slot, value) for slot, value in zip(slots, apply(slots, turns))]
    last = (1, 3, 2)
    return pl.pallas_call(
        functools.partial(far_kernel, last, tuple(slot for slot, _ in early)),
        out_shape=jax.ShapeDtypeStruct(columns.shape, columns.dtype),
        in_specs=[hbm] + [vmem] * (2 * len(last) + len(early)),
        out_specs=hbm,
        scratch_shapes=[
            pltpu.VMEM((len(last), 256, rows_here), jnp.float32),
            pltpu.SMEM(seating.shape, seating.dtype),
            pltpu.SemaphoreType.DMA((2 * SPREAD, 4)),
            pltpu.SemaphoreType.DMA,
        ],
        compiler_params=params(10),
        name="apply_far",
    )(seating, *[far[slot] for slot in last], *[panels[slot] for slot in last], *[value for _, value in early])


def solution(mesh):
    in_specs = (P(None, AXES), P())
    out_specs = P(None, AXES)
    return jax.shard_map(steps, mesh=mesh, in_specs=in_specs, out_specs=out_specs, check_vma=False)
```
